32 devices in a mesh: gx: 16 (over z, y, x), gy: 2 (over core).
Axes of the slice: x: 2, y: 2, z: 4, core: 2. Of those that a mesh axis runs over, the one named last changes fastest.
Arguments:
- coarse_state: float32 [24, 256, 256], P(None, 'gx', 'gy'), may hold values from -6 to 6
- coarse_rate: float32 [256, 256], P('gx', 'gy'), may hold values from 0.5 to 2
- fine_state: float32 [128, 24, 16, 256], P(('gx', 'gy')), may hold values from -6 to 6
- fine_rate: float32 [128, 16, 256], P(('gx', 'gy')), may hold values from 0.5 to 2
- refine_to: int32 [128], P(('gx', 'gy')), may hold values from -1 to 3, as said below
- parent_of: int32 [128], P(('gx', 'gy')), may hold values from -1 to 3, as said below
- kappa: float32 [24], replicated, may hold values from 0.01 to 0.05
- reaction: float32 [24, 24], replicated, may hold values from -1.25 to 1.25
Outputs:
- coarse_out: float32 [24, 256, 256], P(None, 'gx', 'gy')
- fine_out: float32 [128, 24, 16, 256], P(('gx', 'gy'))
The draws below stay inside these ranges and needn't reach their ends.
Inputs may be any that keep to these rules, and one draw needn't show every extreme that they name: `refine_to`: -1 for a parent that is not refined; else k, the slot of its fine patch on the device k // 2 places higher along gx (wrapping), same gy index; no two parents name the same slot. `parent_of`: -1 for an empty slot; else p, its parent on the device k // 2 places lower along gx (wrapping), same gy index, k being the slot within its device; the two maps are inverse to each other; a device holds up to 4 live slots and in every draw some device holds that many.
All inputs are finite; a program needn't handle non-finite values.
Results may differ from the reference program's by a relative error of at most 0.0003.
Values sent between devices are 32-bit elements; how exact they have to be, the bound alone decides.
A program may use at most 64 MiB of HBM per device.

```python
import math
import jax
import jax.numpy as jnp
from jax import lax

F = 24
CX = 16
CY = 16
NZ = 8
REACH = 2
PAR_DEV = 4
SUBSTEPS = 4
NX = 256
NY = 32
FZ = 16
PARENTS = 128
SLOT_DEV = 4
SLOTS = 128
N_GX = 16
N_GY = 2
DEVICES = 32


def build_maps(key):
    base_key = jax.random.fold_in(key, 11)
    key_busy, key_pick, key_order, key_live = jax.random.split(base_key, 4)
    busy_column = jax.random.randint(key_busy, (N_GY,), 0, N_GX)
    gx_column = jnp.arange(N_GX, dtype=jnp.int32)[:, None]
    needed = (busy_column[None, :] - gx_column) % N_GX
    pair_ids = jnp.arange(2 * REACH, dtype=jnp.int32)
    required = pair_ids[None, None, :] // 2 == needed[:, :, None]
    noise_bits = jax.random.randint(key_pick, (N_GX, N_GY, 2 * REACH), 0, 1 << 20)
    scores = noise_bits * (2 * REACH) + pair_ids + required.astype(jnp.int32) * (1 << 28)
    ranked = jnp.argsort(-scores, axis=-1)[..., :PAR_DEV]
    order_bits = jax.random.randint(key_order, (N_GX, N_GY, PAR_DEV), 0, 1 << 20) * PAR_DEV + jnp.arange(PAR_DEV, dtype=jnp.int32)
    shuffle = jnp.argsort(order_bits, axis=-1)
    chosen = jnp.take_along_axis(ranked, shuffle, axis=-1).astype(jnp.int32)
    is_required = chosen // 2 == needed[:, :, None]
    is_live = is_required | (jax.random.randint(key_live, (N_GX, N_GY, PAR_DEV), 0, 4) > 0)
    refine = jnp.where(is_live, chosen, -1)
    matches = (chosen[..., :, None] == pair_ids) & is_live[..., None]
    parent_table = jnp.where(jnp.any(matches, axis=2), jnp.sum(matches.astype(jnp.int32) * jnp.arange(PAR_DEV, dtype=jnp.int32)[:, None], axis=2), -1)
    sources = (gx_column - pair_ids[None, :] // 2) % N_GX
    parents = parent_table[sources[:, None, :], jnp.arange(N_GY, dtype=jnp.int32)[None, :, None], pair_ids[None, None, :]]
    return (refine.reshape(-1).astype(jnp.int32), parents.reshape(-1).astype(jnp.int32))


def draw_refine_to(key, part):
    return build_maps(key)[0]


def draw_parent_of(key, part):
    return build_maps(key)[1]


def block_scale(own_key, extent, shards, smallest, top_value):
    def one(dim, shards_of):
        draws = jax.random.uniform(jax.random.fold_in(jax.random.fold_in(own_key, 6), dim), (shards_of,), jnp.float32, smallest / len(shards), top_value / len(shards))
        return jnp.repeat(jnp.exp(draws), extent[dim] // shards_of).reshape((-1,) + (1,) * (len(extent) - dim - 1))

    gain = one(*shards[0])
    for cut in shards[1:]:
        gain = gain * one(*cut)
    return gain


def normal_values(rng, shape, deviation, limit, shards=(), kind=jnp.bfloat16):
    values = jax.random.normal(rng, shape, jnp.float32) * deviation
    if len(shards) > 0:
        values = block_scale(rng, shape, shards, -0.22, 0.18) * values
    return jnp.clip(values, min=-limit, max=limit).astype(kind)


def setup_inputs(seed: int = 0) -> dict:
    key_list = jax.random.split(jax.random.key(seed), 9)
    coarse_state = normal_values(key_list[0], (F, NX, NY * NZ), 1.0, 6.0, ((1, 16), (2, 2)), jnp.float32)
    coarse_rate = jnp.clip(jnp.exp(math.log(2.0) - 1.3862944 * jax.random.uniform(key_list[1], (NX, NY * NZ), jnp.float32) ** block_scale(key_list[1], (NX, NY * NZ), ((0, 16), (1, 2)), -0.2, 0.2)), 0.5, 2.0)
    fine_state = normal_values(key_list[2], (SLOTS, F, CX, CY * FZ), 1.0, 6.0, ((0, 32),), jnp.float32)
    fine_rate = jnp.clip(jnp.exp(math.log(2.0) - 1.3862944 * jax.random.uniform(key_list[3], (SLOTS, CX, CY * FZ), jnp.float32) ** block_scale(key_list[3], (SLOTS, CX, CY * FZ), ((0, 32),), -0.2, 0.2)), 0.5, 2.0)
    refine_to = draw_refine_to(jax.random.fold_in(key_list[8], 71), 0)
    parent_of = draw_parent_of(jax.random.fold_in(key_list[8], 71), 0)
    kappa = jnp.clip(jnp.exp(jax.random.uniform(key_list[6], (F,), jnp.float32, math.log(0.01), math.log(0.05))), 0.01, 0.05)
    reaction = normal_values(key_list[7], (F, F), F ** -0.5, 1.25, (), jnp.float32)
    return dict(coarse_state=coarse_state, coarse_rate=coarse_rate, fine_state=fine_state, fine_rate=fine_rate, refine_to=refine_to, parent_of=parent_of, kappa=kappa, reaction=reaction)


highest_mode = lax.Precision.HIGHEST


def transport(padded, diffusion, courant):
    center = padded[..., 1:-1, 1:-1, :]
    lateral = padded[..., 2:, 1:-1, :] + padded[..., :-2, 1:-1, :] + padded[..., 1:-1, 2:, :] + padded[..., 1:-1, :-2, :]
    lower_z = jnp.roll(center, 1, axis=-1)
    upper_z = jnp.roll(center, -1, axis=-1)
    laplacian = lateral + lower_z + upper_z - 6.0 * center
    return center + diffusion * laplacian - courant * (center - lower_z)


def react(fields, rate_field, time_step, reaction):
    for substep in range(SUBSTEPS):
        fields = fields + (time_step / SUBSTEPS) * rate_field * jnp.einsum("fg,...gxyz->...fxyz", reaction, fields, precision=highest_mode)
    return fields


def fine_steps(patches, patch_rates, cycle_old, cycle_mid, kappa, reaction):
    for cycle_now in (cycle_old, cycle_mid):
        upsampled = jnp.repeat(jnp.repeat(jnp.repeat(cycle_now, 2, axis=-3), 2, axis=-2), 2, axis=-1)
        padded = upsampled[..., 1:-1, 1:-1, :].at[..., 1:-1, 1:-1, :].set(patches)
        patches = react(transport(padded, 2.0 * kappa[:, None, None, None], 0.25), patch_rates[:, None], 0.5, reaction)
    return patches


def coarse_means(patches):
    count, fields, size_x, size_y, size_z = patches.shape
    return patches.reshape(count, fields, size_x // 2, 2, size_y // 2, 2, size_z // 2, 2).mean(axis=(3, 5, 7))


def reference(coarse_state, coarse_rate, fine_state, fine_rate, refine_to, parent_of, kappa, reaction):
    half_x = CX // 2
    half_y = CY // 2
    fine_z = 2 * NZ
    coarse_grid = coarse_state.reshape(F, NX, NY, NZ)
    rate_grid = coarse_rate.reshape(NX, NY, NZ)
    diffusion = kappa[:, None, None, None]
    wrap_pad = ((0, 0), (1, 1), (1, 1), (0, 0))
    padded_old = jnp.pad(coarse_grid, wrap_pad, mode="wrap")
    coarse_new = react(transport(padded_old, diffusion, 0.25), rate_grid, 1.0, reaction)
    padded_new = jnp.pad(coarse_new, wrap_pad, mode="wrap")

    def cut_cycle(field, start_x, start_y):
        return lax.dynamic_slice(field, (jnp.int32(0), start_x, start_y, jnp.int32(0)), (F, half_x + 2, half_y + 2, NZ))

    def one_device(inputs):
        patches, patch_rates, parents, device = inputs
        gx_index = device // N_GY
        gy_index = device % N_GY
        slot_ids = jnp.arange(SLOT_DEV, dtype=jnp.int32)
        sources = (gx_index - slot_ids // 2) % N_GX
        chosen = jnp.maximum(parents, 0)
        starts_x = (sources * CX + half_x * (chosen // 2)).astype(jnp.int32)
        starts_y = (gy_index * CY + half_y * (chosen % 2)).astype(jnp.int32)
        cycle_old = jax.vmap(cut_cycle, in_axes=(None, 0, 0))(padded_old, starts_x, starts_y)
        cycle_new = jax.vmap(cut_cycle, in_axes=(None, 0, 0))(padded_new, starts_x, starts_y)
        advanced = fine_steps(patches, patch_rates, cycle_old, 0.5 * (cycle_old + cycle_new), kappa, reaction)
        is_live = parents >= 0
        finished = jnp.where(is_live[:, None, None, None, None], advanced, 0.0)
        return finished, coarse_means(finished)

    device_ids = jnp.arange(DEVICES, dtype=jnp.int32)
    fine_out, averages = lax.map(one_device, (fine_state.reshape(DEVICES, SLOT_DEV, F, CX, CY, fine_z), fine_rate.reshape(DEVICES, SLOT_DEV, CX, CY, fine_z), parent_of.reshape(DEVICES, SLOT_DEV), device_ids))
    fine_out = fine_out.reshape(fine_state.shape)
    averages = averages.reshape(SLOTS, F, half_x, half_y, NZ)
    parent_ids = jnp.arange(PARENTS, dtype=jnp.int32)
    home_device = parent_ids // PAR_DEV
    gx_home = home_device // N_GY
    gy_home = home_device % N_GY
    chosen = jnp.maximum(refine_to, 0)
    owner_device = ((gx_home + chosen // 2) % N_GX) * N_GY + gy_home
    averaged = averages[(owner_device * SLOT_DEV + chosen).astype(jnp.int32)]
    coarse_parts = coarse_new.reshape(F, N_GX, 2, half_x, N_GY, 2, half_y, NZ).transpose(1, 4, 2, 5, 0, 3, 6, 7).reshape(PARENTS, F, half_x, half_y, NZ)
    merged = jnp.where((refine_to >= 0)[:, None, None, None, None], averaged, coarse_parts)
    coarse_out = merged.reshape(N_GX, N_GY, 2, 2, F, half_x, half_y, NZ).transpose(4, 0, 2, 5, 1, 3, 6, 7).reshape(coarse_state.shape)
    return coarse_out, fine_out
```

```python
import functools
import jax
import jax.numpy as jnp
from jax import lax
from jax.experimental import pallas as pl
from jax.experimental.pallas import tpu as pltpu
from jax.sharding import PartitionSpec as P

MESH = pl.DeviceIdType.MESH
F32 = jnp.float32
BF16 = jnp.bfloat16


def lanes(rows):
    return lax.broadcasted_iota(jnp.int32, (rows, 128), 1)


def pick(table, index):
    return jnp.take_along_axis(table, index, axis=1)


def powers(reaction, fields):
    row = lax.broadcasted_iota(jnp.int32, (fields, 3 * fields), 0)
    col = lax.broadcasted_iota(jnp.int32, (fields, 3 * fields), 1)
    power = (col % fields == row).astype(F32)
    result = []
    for _ in range(4):
        power = jnp.dot(
            reaction, power, precision=lax.Precision.HIGHEST, preferred_element_type=F32
        )
        result.append(power)
    return result, col < 2 * fields


def chem_weights(power_list, high_part, step):
    parts = []
    for count, (choose, power) in enumerate(zip((4.0, 6.0, 4.0, 1.0), power_list)):
        value = power * (choose * step ** (count + 1))
        high = value.astype(BF16).astype(F32)
        parts.append(jnp.where(high_part, high, value - high))
    return jnp.concatenate(parts, axis=0).astype(BF16)


def chemistry(weights, values, rates, fields):
    wide = jnp.concatenate(values, axis=1)
    high = wide.astype(BF16).astype(F32)
    low = wide - high
    stacked = jnp.concatenate([high, low, high], axis=0).astype(BF16)
    product = jnp.dot(weights, stacked, preferred_element_type=F32)
    out = []
    for n, (value, rate) in enumerate(zip(values, rates)):
        part = [
            product[q * fields : (q + 1) * fields, n * 128 : (n + 1) * 128] for q in range(4)
        ]
        rate = jnp.broadcast_to(rate, value.shape)
        out.append(value + rate * (part[0] + rate * (part[1] + rate * (part[2] + rate * part[3]))))
    return out


def kernel(
    n_gx, n_gy, fields, size_x, slots,
    refine_ref, parent_ref, coarse_hbm, crate_hbm, fine_hbm, frate_hbm, kappa_ref, reaction_ref,
    coarse_out_hbm, fine_out_hbm,
    cin, crate, fin, frate, fout, cout,
    buf_a, buf_b, row_send, col_send, hx, hy, cnew, cols, ring_local, ring_send, ring_recv,
    means, mean_send, mean_recv, wf_ref, wc_ref, rate8,
    in_sem, out_sem, send_sem, recv_sem,
):
    F = fields
    gx = lax.axis_index("gx")
    gy = lax.axis_index("gy")
    right = lax.rem(gx + 1, n_gx)
    left = lax.rem(gx + n_gx - 1, n_gx)
    above = lax.rem(gy + 1, n_gy)
    below = lax.rem(gy + n_gy - 1, n_gy)

    loads = [
        pltpu.make_async_copy(coarse_hbm, cin, in_sem.at[0]),
        pltpu.make_async_copy(crate_hbm, crate, in_sem.at[1]),
        pltpu.make_async_copy(frate_hbm, frate, in_sem.at[2]),
    ]
    fine_loads = []
    for s in range(slots):
        for h in range(2):
            fine_loads.append(
                pltpu.make_async_copy(
                    fine_hbm.at[s, :, pl.ds(h * 128, 128)], fin.at[s, h], in_sem.at[3 + 2 * s + h]
                )
            )
    for copy in loads + fine_loads:
        copy.start()

    barrier = pltpu.get_barrier_semaphore()
    for target in ((left, gy), (right, gy), (gx, below), (gx, above)):
        pl.semaphore_signal(barrier, inc=1, device_id=target, device_id_type=MESH)

    def send(n, src, dst, target):
        copy = pltpu.make_async_remote_copy(
            src_ref=src, dst_ref=dst, send_sem=send_sem.at[n], recv_sem=recv_sem.at[n],
            device_id=target, device_id_type=MESH,
        )
        copy.start()
        return copy

    lane = lanes(F)
    first_half = lane < 64

    def pack(rows_of, y):
        total = jnp.zeros((F, 128), F32)
        for x in range(size_x):
            shift = ((x - y) * 8) % 128
            row = rows_of(x)
            moved = pltpu.roll(row, shift, 1) if shift else row
            total = jnp.where(lane // 8 == x, moved, total)
        return total

    def halos(level):
        base = 4 * level
        return [
            send(base + 0, row_send.at[level, 1], hx.at[level, 0], (right, gy)),
            send(base + 1, row_send.at[level, 0], hx.at[level, 1], (left, gy)),
            send(base + 2, col_send.at[level, 1], hy.at[level, 0], (gx, above)),
            send(base + 3, col_send.at[level, 0], hy.at[level, 1], (gx, below)),
        ]

    loads[0].wait()
    old_rows = lambda x: cin[pl.ds(x, F, stride=size_x), :]
    row_send[0, 0] = old_rows(0)
    row_send[0, 1] = old_rows(size_x - 1)
    col_send[0, 0] = pack(old_rows, 0)
    col_send[0, 1] = pack(old_rows, size_x - 1)
    pl.semaphore_wait(barrier, 4)
    pending = halos(0)
    old_halos = pending

    cols[0, 0] = pack(old_rows, size_x // 2 - 1)
    cols[0, 1] = pack(old_rows, size_x // 2)
    power_list, high_part = powers(reaction_ref[...], F)
    wf_ref[...] = chem_weights(power_list, high_part, 0.125)
    wc_ref[...] = chem_weights(power_list, high_part, 0.25)
    diag = lax.broadcasted_iota(jnp.int32, (F, F), 0) == lax.broadcasted_iota(jnp.int32, (F, F), 1)
    kappa_col = jnp.sum(
        jnp.where(diag, jnp.broadcast_to(kappa_ref[...], (F, F)), 0.0), axis=1, keepdims=True
    )
    kappa = jnp.broadcast_to(kappa_col, (F, 128))
    kappa2 = 2.0 * kappa

    for copy in fine_loads:
        copy.wait()
    for s in range(slots):
        for h in range(2):
            for x in range(size_x):
                buf_a[s, x + 1, :, pl.ds(h * 128, 128)] = fin[s, h, pl.ds(x, F, stride=size_x), :]
    loads[1].wait()
    loads[2].wait()
    for s in range(slots):
        for x in range(size_x):
            rate8[s, x] = jnp.broadcast_to(frate[s, pl.ds(x, 1), :], rate8.shape[2:])

    for copy in old_halos:
        copy.wait_recv()

    z8 = lane % 8
    for group in range(size_x // 4):
        values, rates = [], []
        for x in range(4 * group, 4 * group + 4):
            c = old_rows(x)
            up = old_rows(x - 1) if x > 0 else hx[0, 0]
            dn = old_rows(x + 1) if x < size_x - 1 else hx[0, 1]
            ghost_lo = pltpu.roll(hy[0, 0], (-x * 8) % 128, 1) if x else hy[0, 0]
            shift = (120 - x * 8) % 128
            ghost_hi = pltpu.roll(hy[0, 1], shift, 1) if shift else hy[0, 1]
            yl = jnp.where(lane < 8, ghost_lo, pltpu.roll(c, 8, 1))
            yh = jnp.where(lane >= 120, ghost_hi, pltpu.roll(c, 120, 1))
            zl = jnp.where(z8 == 0, pltpu.roll(c, 121, 1), pltpu.roll(c, 1, 1))
            zu = jnp.where(z8 == 7, pltpu.roll(c, 7, 1), pltpu.roll(c, 127, 1))
            lap = (yl + yh) + (up + dn) + (zl + zu) - 6.0 * c
            values.append(c + kappa * lap - 0.25 * (c - zl))
            rates.append(crate[pl.ds(x, 1), :])
        for n, new in enumerate(chemistry(wc_ref[...], values, rates, F)):
            cnew[4 * group + n] = new
    new_rows = lambda x: cnew[x]
    row_send[1, 0] = new_rows(0)
    row_send[1, 1] = new_rows(size_x - 1)
    col_send[1, 0] = pack(new_rows, 0)
    col_send[1, 1] = pack(new_rows, size_x - 1)
    new_halos = halos(1)

    parents = [jnp.full((F, 128), refine_ref[p], jnp.int32) for p in range(4)]

    def rings(level, rows_of):
        mid = size_x // 2
        row_at = (hx[level, 0], rows_of(mid - 1), rows_of(mid), hx[level, 1])
        col_at = (hy[level, 0], cols[level, 0], cols[level, 1], hy[level, 1])

        def joined(lo, hi, half):
            if half == 0:
                return jnp.where(first_half, lo, pltpu.roll(hi, 64, 1))
            return jnp.where(first_half, pltpu.roll(lo, 64, 1), hi)

        all_rings = []
        for p in range(4):
            a, b = p // 2, p % 2
            all_rings.append(
                (joined(row_at[a], row_at[a + 2], b), joined(col_at[b], col_at[b + 2], a))
            )
        for k in range(4):
            for side in range(2):
                value = jnp.zeros((F, 128), F32)
                for p in range(4):
                    value = jnp.where(parents[p] == k, all_rings[p][side], value)
                if k < 2:
                    ring_local[level, k, side] = value
                else:
                    ring_send[level, k - 2, side] = value
        return send(8 + level, ring_send.at[level], ring_recv.at[level], (right, gy))

    ring_old = rings(0, old_rows)
    cols[1, 0] = pack(new_rows, size_x // 2 - 1)
    cols[1, 1] = pack(new_rows, size_x // 2)

    z16 = lane % 16
    row_index = (lane // 32) * 8 + z16 // 2
    col_index = jnp.where(lane < 64, 0, 64) + z16 // 2
    target = lane % 64
    mean_index = ((target // 8) % 4) * 32 + 2 * (target % 8)
    mean_low = target // 32 == 0

    def ring_of(level, s, side):
        return ring_local[level, s, side] if s < 2 else ring_recv[level, s - 2, side]

    def fine_step(s, step):
        src = buf_a if step == 0 else buf_b
        if step == 0:
            edge_x, edge_y = ring_of(0, s, 0), ring_of(0, s, 1)
        else:
            edge_x = 0.5 * (ring_of(0, s, 0) + ring_of(1, s, 0))
            edge_y = 0.5 * (ring_of(0, s, 1) + ring_of(1, s, 1))
        for h in range(2):
            src[s, 0, :, pl.ds(h * 128, 128)] = pick(edge_x, row_index + 32 * h)
            src[s, size_x + 1, :, pl.ds(h * 128, 128)] = pick(edge_x, row_index + 64 + 32 * h)
        weights = wf_ref[...]
        live = jnp.full((F, 128), parent_ref[s], jnp.int32) >= 0

        def pair(j, carry):
            ghost = pick(edge_y, col_index + 8 * j)
            values, rates = [], []
            for n in range(2):
                x = 2 * j + n
                c = [src[s, x + 1, :, pl.ds(h * 128, 128)] for h in range(2)]
                up = [src[s, x, :, pl.ds(h * 128, 128)] for h in range(2)]
                dn = [src[s, x + 2, :, pl.ds(h * 128, 128)] for h in range(2)]
                ra = [pltpu.roll(v, 16, 1) for v in c]
                rb = [pltpu.roll(v, 112, 1) for v in c]
                yl = [jnp.where(lane < 16, ghost, ra[0]), jnp.where(lane < 16, ra[0], ra[1])]
                yh = [jnp.where(lane >= 112, rb[1], rb[0]), jnp.where(lane >= 112, ghost, rb[1])]
                for h in range(2):
                    v = c[h]
                    zl = jnp.where(z16 == 0, pltpu.roll(v, 113, 1), pltpu.roll(v, 1, 1))
                    zu = jnp.where(z16 == 15, pltpu.roll(v, 15, 1), pltpu.roll(v, 127, 1))
                    lap = (yl[h] + yh[h]) + (up[h] + dn[h]) + (zl + zu) - 6.0 * v
                    values.append(v + kappa2 * lap - 0.25 * (v - zl))
                    rate = rate8[s, x, :, pl.ds(h * 128, 128)]
                    rates.append(jnp.concatenate([rate] * (F // 8), axis=0))
            new = chemistry(weights, values, rates, F)
            if step == 0:
                for n in range(2):
                    for h in range(2):
                        buf_b[s, 2 * j + n + 1, :, pl.ds(h * 128, 128)] = new[2 * n + h]
            else:
                new = [jnp.where(live, v, 0.0) for v in new]
                for n in range(2):
                    for h in range(2):
                        fout[s, h, pl.ds(2 * j + n, F, stride=size_x), :] = new[2 * n + h]
                picked = []
                for h in range(2):
                    total = new[h] + new[2 + h]
                    total = total + pltpu.roll(total, 127, 1)
                    total = total + pltpu.roll(total, 112, 1)
                    picked.append(pick(total, mean_index))
                means[s, j] = 0.125 * jnp.where(mean_low, picked[0], picked[1])
            return carry

        lax.fori_loop(0, size_x // 2, pair, 0)

    stores = []

    def store(s):
        for h in range(2):
            copy = pltpu.make_async_copy(
                fout.at[s, h], fine_out_hbm.at[s, :, pl.ds(h * 128, 128)], out_sem.at[2 * s + h]
            )
            copy.start()
            stores.append(copy)

    half = size_x // 4

    def send_means(s):
        for j in range(half):
            mean_send[s - 2, j] = jnp.where(first_half, means[s, j], means[s, j + half])
        return send(8 + s, mean_send.at[s - 2], mean_recv.at[s - 2], (left, gy))

    fine_step(0, 0)
    fine_step(1, 0)
    for copy in new_halos:
        copy.wait_recv()
    ring_new = rings(1, new_rows)
    fine_step(0, 1)
    store(0)
    ring_old.wait_recv()
    fine_step(2, 0)
    fine_step(3, 0)
    ring_new.wait_recv()
    fine_step(2, 1)
    sent_2 = send_means(2)
    store(2)
    fine_step(3, 1)
    sent_3 = send_means(3)
    store(3)
    fine_step(1, 1)
    store(1)
    sent_2.wait_recv()
    sent_3.wait_recv()

    for x in range(size_x):
        a, X = x // (size_x // 2), x % (size_x // 2)
        full = [means[0, X], means[1, X]]
        for k in range(2):
            packed = mean_recv[k, X % half]
            turned = pltpu.roll(packed, 64, 1)
            low, high = (packed, turned) if X < half else (turned, packed)
            full.append(jnp.where(first_half, low, high))
        owner = jnp.where(first_half, parents[2 * a], parents[2 * a + 1])
        value = new_rows(x)
        for k in range(4):
            value = jnp.where(owner == k, full[k], value)
        cout[pl.ds(x, F, stride=size_x), :] = value
    last = pltpu.make_async_copy(cout, coarse_out_hbm, out_sem.at[8])
    last.start()
    stores.append(last)
    for copy in old_halos + new_halos + [ring_old, ring_new, sent_2, sent_3]:
        copy.wait_send()
    for copy in stores:
        copy.wait()


def body(coarse_state, coarse_rate, fine_state, fine_rate, refine_to, parent_of, kappa, reaction):
    fields, size_x, merged = coarse_state.shape
    slots = fine_state.shape[0]
    fine_merged = fine_state.shape[3]
    flat = fields * size_x
    any_spec = pl.BlockSpec(memory_space=pl.ANY)
    smem = pl.BlockSpec(memory_space=pltpu.SMEM)
    vmem = pl.BlockSpec(memory_space=pltpu.VMEM)
    V = pltpu.VMEM
    tile = (fields, 128)
    coarse_out, fine_out = pl.pallas_call(
        functools.partial(
            kernel, lax.axis_size("gx"), lax.axis_size("gy"), fields, size_x, slots
        ),
        out_shape=(
            jax.ShapeDtypeStruct((flat, merged), F32),
            jax.ShapeDtypeStruct((slots, flat, fine_merged), F32),
        ),
        in_specs=[smem, smem, any_spec, any_spec, any_spec, any_spec, vmem, vmem],
        out_specs=(any_spec, any_spec),
        scratch_shapes=[
            V((flat, 128), F32),
            V((size_x, 128), F32),
            V((slots, 2, flat, 128), F32),
            V((slots, size_x, fine_merged), F32),
            V((slots, 2, flat, 128), F32),
            V((flat, 128), F32),
            V((slots, size_x + 2, fields, fine_merged), F32),
            V((slots, size_x + 2, fields, fine_merged), F32),
            V((2, 2) + tile, F32),
            V((2, 2) + tile, F32),
            V((2, 2) + tile, F32),
            V((2, 2) + tile, F32),
            V((size_x,) + tile, F32),
            V((2, 2) + tile, F32),
            V((2, 2, 2) + tile, F32),
            V((2, 2, 2) + tile, F32),
            V((2, 2, 2) + tile, F32),
            V((slots, size_x // 2) + tile, F32),
            V((2, size_x // 4) + tile, F32),
            V((2, size_x // 4) + tile, F32),
            V((4 * fields, 3 * fields), BF16),
            V((4 * fields, 3 * fields), BF16),
            V((slots, size_x, 8, fine_merged), F32),
            pltpu.SemaphoreType.DMA((11,)),
            pltpu.SemaphoreType.DMA((9,)),
            pltpu.SemaphoreType.DMA((12,)),
            pltpu.SemaphoreType.DMA((12,)),
        ],
        compiler_params=pltpu.CompilerParams(
            collective_id=0, has_side_effects=True, vmem_limit_bytes=48 * 1024 * 1024
        ),
    )(
        refine_to, parent_of, coarse_state.reshape(flat, merged), coarse_rate,
        fine_state.reshape(slots, flat, fine_merged), fine_rate, kappa.reshape(1, fields), reaction,
    )
    return coarse_out.reshape(coarse_state.shape), fine_out.reshape(fine_state.shape)


def solution(mesh):
    in_specs = (
        P(None, "gx", "gy"),
        P("gx", "gy"),
        P(("gx", "gy"), None, None, None),
        P(("gx", "gy"), None, None),
        P(("gx", "gy")),
        P(("gx", "gy")),
        P(),
        P(),
    )
    out_specs = (P(None, "gx", "gy"), P(("gx", "gy"), None, None, None))
    return jax.shard_map(body, mesh=mesh, in_specs=in_specs, out_specs=out_specs, check_vma=False)
```

```python
import functools
import jax
import jax.numpy as jnp
from jax import lax
from jax.experimental import pallas as pl
from jax.experimental.pallas import tpu as pltpu
from jax.sharding import PartitionSpec as P

MESH = pl.DeviceIdType.MESH
F32 = jnp.float32
BF16 = jnp.bfloat16


def lanes(rows):
    return lax.broadcasted_iota(jnp.int32, (rows, 128), 1)


def pick(table, index):
    return jnp.take_along_axis(table, index, axis=1)


def powers(reaction, fields):
    row = lax.broadcasted_iota(jnp.int32, (fields, 3 * fields), 0)
    col = lax.broadcasted_iota(jnp.int32, (fields, 3 * fields), 1)
    power = (col % fields == row).astype(F32)
    result = []
    for _ in range(4):
        power = jnp.dot(
            reaction, power, precision=lax.Precision.HIGHEST, preferred_element_type=F32
        )
        result.append(power)
    return result, col < 2 * fields


def chem_weights(power_list, high_part, step):
    parts = []
    for count, (choose, power) in enumerate(zip((4.0, 6.0, 4.0, 1.0), power_list)):
        value = power * (choose * step ** (count + 1))
        high = value.astype(BF16).astype(F32)
        parts.append(jnp.where(high_part, high, value - high))
    return jnp.concatenate(parts, axis=0).astype(BF16)


def chemistry(weights, values, rates, fields):
    wide = jnp.concatenate(values, axis=1)
    high = wide.astype(BF16).astype(F32)
    low = wide - high
    stacked = jnp.concatenate([high, low, high], axis=0).astype(BF16)
    product = jnp.dot(weights, stacked, preferred_element_type=F32)
    out = []
    for n, (value, rate) in enumerate(zip(values, rates)):
        part = [
            product[q * fields : (q + 1) * fields, n * 128 : (n + 1) * 128] for q in range(4)
        ]
        rate = jnp.broadcast_to(rate, value.shape)
        out.append(value + rate * (part[0] + rate * (part[1] + rate * (part[2] + rate * part[3]))))
    return out


def kernel(
    n_gx, n_gy, fields, size_x, slots,
    refine_ref, parent_ref, coarse_hbm, crate_hbm, fine_hbm, frate_hbm, kappa_ref, reaction_ref,
    coarse_out_hbm, fine_out_hbm,
    cin, crate, fin, frate, fout, cout,
    buf_a, buf_b, row_send, col_send, hx, hy, cnew, cols, ring_local, ring_send, ring_recv,
    means, mean_send, mean_recv, wf_ref, wc_ref, rate8,
    in_sem, out_sem, send_sem, recv_sem,
):
    F = fields
    gx = lax.axis_index("gx")
    gy = lax.axis_index("gy")
    right = lax.rem(gx + 1, n_gx)
    left = lax.rem(gx + n_gx - 1, n_gx)
    above = lax.rem(gy + 1, n_gy)
    below = lax.rem(gy + n_gy - 1, n_gy)

    loads = [
        pltpu.make_async_copy(coarse_hbm, cin, in_sem.at[0]),
        pltpu.make_async_copy(crate_hbm, crate, in_sem.at[1]),
        pltpu.make_async_copy(frate_hbm, frate, in_sem.at[2]),
    ]
    fine_loads = []
    for s in range(slots):
        for h in range(2):
            fine_loads.append(
                pltpu.make_async_copy(
                    fine_hbm.at[s, :, pl.ds(h * 128, 128)], fin.at[s, h], in_sem.at[3 + 2 * s + h]
                )
            )
    for copy in loads + fine_loads:
        copy.start()

    barrier = pltpu.get_barrier_semaphore()
    for target in ((left, gy), (right, gy), (gx, below), (gx, above)):
        pl.semaphore_signal(barrier, inc=1, device_id=target, device_id_type=MESH)

    def send(n, src, dst, target):
        copy = pltpu.make_async_remote_copy(
            src_ref=src, dst_ref=dst, send_sem=send_sem.at[n], recv_sem=recv_sem.at[n],
            device_id=target, device_id_type=MESH,
        )
        copy.start()
        return copy

    lane = lanes(F)
    first_half = lane < 64

    def pack(rows_of, y):
        total = jnp.zeros((F, 128), F32)
        for x in range(size_x):
            shift = ((x - y) * 8) % 128
            row = rows_of(x)
            moved = pltpu.roll(row, shift, 1) if shift else row
            total = jnp.where(lane // 8 == x, moved, total)
        return total

    def halos(level):
        base = 4 * level
        return [
            send(base + 0, row_send.at[level, 1], hx.at[level, 0], (right, gy)),
            send(base + 1, row_send.at[level, 0], hx.at[level, 1], (left, gy)),
            send(base + 2, col_send.at[level, 1], hy.at[level, 0], (gx, above)),
            send(base + 3, col_send.at[level, 0], hy.at[level, 1], (gx, below)),
        ]

    loads[0].wait()
    old_rows = lambda x: cin[pl.ds(x, F, stride=size_x), :]
    row_send[0, 0] = old_rows(0)
    row_send[0, 1] = old_rows(size_x - 1)
    col_send[0, 0] = pack(old_rows, 0)
    col_send[0, 1] = pack(old_rows, size_x - 1)
    pl.semaphore_wait(barrier, 4)
    pending = halos(0)
    old_halos = pending

    cols[0, 0] = pack(old_rows, size_x // 2 - 1)
    cols[0, 1] = pack(old_rows, size_x // 2)
    power_list, high_part = powers(reaction_ref[...], F)
    wf_ref[...] = chem_weights(power_list, high_part, 0.125)
    wc_ref[...] = chem_weights(power_list, high_part, 0.25)
    diag = lax.broadcasted_iota(jnp.int32, (F, F), 0) == lax.broadcasted_iota(jnp.int32, (F, F), 1)
    kappa_col = jnp.sum(
        jnp.where(diag, jnp.broadcast_to(kappa_ref[...], (F, F)), 0.0), axis=1, keepdims=True
    )
    kappa = jnp.broadcast_to(kappa_col, (F, 128))
    kappa2 = 2.0 * kappa

    for copy in fine_loads:
        copy.wait()
    for s in range(slots):
        for h in range(2):
            for x in range(size_x):
                buf_a[s, x + 1, :, pl.ds(h * 128, 128)] = fin[s, h, pl.ds(x, F, stride=size_x), :]
    loads[1].wait()
    loads[2].wait()
    for s in range(slots):
        for x in range(size_x):
            rate8[s, x] = jnp.broadcast_to(frate[s, pl.ds(x, 1), :], rate8.shape[2:])

    for copy in old_halos:
        copy.wait_recv()

    z8 = lane % 8
    for group in range(size_x // 4):
        values, rates = [], []
        for x in range(4 * group, 4 * group + 4):
            c = old_rows(x)
            up = old_rows(x - 1) if x > 0 else hx[0, 0]
            dn = old_rows(x + 1) if x < size_x - 1 else hx[0, 1]
            ghost_lo = pltpu.roll(hy[0, 0], (-x * 8) % 128, 1) if x else hy[0, 0]
            shift = (120 - x * 8) % 128
            ghost_hi = pltpu.roll(hy[0, 1], shift, 1) if shift else hy[0, 1]
            yl = jnp.where(lane < 8, ghost_lo, pltpu.roll(c, 8, 1))
            yh = jnp.where(lane >= 120, ghost_hi, pltpu.roll(c, 120, 1))
            zl = jnp.where(z8 == 0, pltpu.roll(c, 121, 1), pltpu.roll(c, 1, 1))
            zu = jnp.where(z8 == 7, pltpu.roll(c, 7, 1), pltpu.roll(c, 127, 1))
            lap = (yl + yh) + (up + dn) + (zl + zu) - 6.0 * c
            values.append(c + kappa * lap - 0.25 * (c - zl))
            rates.append(crate[pl.ds(x, 1), :])
        for n, new in enumerate(chemistry(wc_ref[...], values, rates, F)):
            cnew[4 * group + n] = new
    new_rows = lambda x: cnew[x]
    row_send[1, 0] = new_rows(0)
    row_send[1, 1] = new_rows(size_x - 1)
    col_send[1, 0] = pack(new_rows, 0)
    col_send[1, 1] = pack(new_rows, size_x - 1)
    new_halos = halos(1)

    parents = [jnp.full((F, 128), refine_ref[p], jnp.int32) for p in range(4)]

    def rings(level, rows_of):
        mid = size_x // 2
        row_at = (hx[level, 0], rows_of(mid - 1), rows_of(mid), hx[level, 1])
        col_at = (hy[level, 0], cols[level, 0], cols[level, 1], hy[level, 1])

        def joined(lo, hi, half):
            if half == 0:
                return jnp.where(first_half, lo, pltpu.roll(hi, 64, 1))
            return jnp.where(first_half, pltpu.roll(lo, 64, 1), hi)

        all_rings = []
        for p in range(4):
            a, b = p // 2, p % 2
            all_rings.append(
                (joined(row_at[a], row_at[a + 2], b), joined(col_at[b], col_at[b + 2], a))
            )
        for k in range(4):
            for side in range(2):
                value = jnp.zeros((F, 128), F32)
                for p in range(4):
                    value = jnp.where(parents[p] == k, all_rings[p][side], value)
                if k < 2:
                    ring_local[level, k, side] = value
                else:
                    ring_send[level, k - 2, side] = value
        return send(8 + level, ring_send.at[level], ring_recv.at[level], (right, gy))

    ring_old = rings(0, old_rows)
    cols[1, 0] = pack(new_rows, size_x // 2 - 1)
    cols[1, 1] = pack(new_rows, size_x // 2)

    z16 = lane % 16
    row_index = (lane // 32) * 8 + z16 // 2
    col_index = jnp.where(lane < 64, 0, 64) + z16 // 2
    target = lane % 64
    mean_index = ((target // 8) % 4) * 32 + 2 * (target % 8)
    mean_low = target // 32 == 0

    def ring_of(level, s, side):
        return ring_local[level, s, side] if s < 2 else ring_recv[level, s - 2, side]

    def fine_step(s, step):
        src = buf_a if step == 0 else buf_b
        if step == 0:
            edge_x, edge_y = ring_of(0, s, 0), ring_of(0, s, 1)
        else:
            edge_x = 0.5 * (ring_of(0, s, 0) + ring_of(1, s, 0))
            edge_y = 0.5 * (ring_of(0, s, 1) + ring_of(1, s, 1))
        for h in range(2):
            src[s, 0, :, pl.ds(h * 128, 128)] = pick(edge_x, row_index + 32 * h)
            src[s, size_x + 1, :, pl.ds(h * 128, 128)] = pick(edge_x, row_index + 64 + 32 * h)
        weights = wf_ref[...]
        live = jnp.full((F, 128), parent_ref[s], jnp.int32) >= 0

        def pair(j, carry):
            ghost = pick(edge_y, col_index + 8 * j)
            values, rates = [], []
            for n in range(2):
                x = 2 * j + n
                c = [src[s, x + 1, :, pl.ds(h * 128, 128)] for h in range(2)]
                up = [src[s, x, :, pl.ds(h * 128, 128)] for h in range(2)]
                dn = [src[s, x + 2, :, pl.ds(h * 128, 128)] for h in range(2)]
                ra = [pltpu.roll(v, 16, 1) for v in c]
                rb = [pltpu.roll(v, 112, 1) for v in c]
                yl = [jnp.where(lane < 16, ghost, ra[0]), jnp.where(lane < 16, ra[0], ra[1])]
                yh = [jnp.where(lane >= 112, rb[1], rb[0]), jnp.where(lane >= 112, ghost, rb[1])]
                for h in range(2):
                    v = c[h]
                    zl = jnp.where(z16 == 0, pltpu.roll(v, 113, 1), pltpu.roll(v, 1, 1))
                    zu = jnp.where(z16 == 15, pltpu.roll(v, 15, 1), pltpu.roll(v, 127, 1))
                    lap = (yl[h] + yh[h]) + (up[h] + dn[h]) + (zl + zu) - 6.0 * v
                    values.append(v + kappa2 * lap - 0.25 * (v - zl))
                    rate = rate8[s, x, :, pl.ds(h * 128, 128)]
                    rates.append(jnp.concatenate([rate] * (F // 8), axis=0))
            new = chemistry(weights, values, rates, F)
            if step == 0:
                for n in range(2):
                    for h in range(2):
                        buf_b[s, 2 * j + n + 1, :, pl.ds(h * 128, 128)] = new[2 * n + h]
            else:
                new = [jnp.where(live, v, 0.0) for v in new]
                for n in range(2):
                    for h in range(2):
                        fout[s, h, pl.ds(2 * j + n, F, stride=size_x), :] = new[2 * n + h]
                picked = []
                for h in range(2):
                    total = new[h] + new[2 + h]
                    total = total + pltpu.roll(total, 127, 1)
                    total = total + pltpu.roll(total, 112, 1)
                    picked.append(pick(total, mean_index))
                means[s, j] = 0.125 * jnp.where(mean_low, picked[0], picked[1])
            return carry

        lax.fori_loop(0, size_x // 2, pair, 0)

    stores = []

    def store(s):
        for h in range(2):
            copy = pltpu.make_async_copy(
                fout.at[s, h], fine_out_hbm.at[s, :, pl.ds(h * 128, 128)], out_sem.at[2 * s + h]
            )
            copy.start()
            stores.append(copy)

    half = size_x // 4

    def send_means(s):
        for j in range(half):
            mean_send[s - 2, j] = jnp.where(first_half, means[s, j], means[s, j + half])
        return send(8 + s, mean_send.at[s - 2], mean_recv.at[s - 2], (left, gy))

    fine_step(0, 0)
    fine_step(1, 0)
    for copy in new_halos:
        copy.wait_recv()
    ring_new = rings(1, new_rows)
    fine_step(0, 1)
    store(0)
    ring_old.wait_recv()
    fine_step(2, 0)
    fine_step(3, 0)
    ring_new.wait_recv()
    fine_step(2, 1)
    sent_2 = send_means(2)
    store(2)
    fine_step(3, 1)
    sent_3 = send_means(3)
    store(3)
    fine_step(1, 1)
    store(1)
    sent_2.wait_recv()
    sent_3.wait_recv()

    for x in range(size_x):
        a, X = x // (size_x // 2), x % (size_x // 2)
        full = [means[0, X], means[1, X]]
        for k in range(2):
            packed = mean_recv[k, X % half]
            turned = pltpu.roll(packed, 64, 1)
            low, high = (packed, turned) if X < half else (turned, packed)
            full.append(jnp.where(first_half, low, high))
        owner = jnp.where(first_half, parents[2 * a], parents[2 * a + 1])
        value = new_rows(x)
        for k in range(4):
            value = jnp.where(owner == k, full[k], value)
        cout[pl.ds(x, F, stride=size_x), :] = value
    last = pltpu.make_async_copy(cout, coarse_out_hbm, out_sem.at[8])
    last.start()
    stores.append(last)
    for copy in old_halos + new_halos + [ring_old, ring_new, sent_2, sent_3]:
        copy.wait_send()
    for copy in stores:
        copy.wait()


def body(coarse_state, coarse_rate, fine_state, fine_rate, refine_to, parent_of, kappa, reaction):
    fields, size_x, merged = coarse_state.shape
    slots = fine_state.shape[0]
    fine_merged = fine_state.shape[3]
    flat = fields * size_x
    any_spec = pl.BlockSpec(memory_space=pl.ANY)
    smem = pl.BlockSpec(memory_space=pltpu.SMEM)
    vmem = pl.BlockSpec(memory_space=pltpu.VMEM)
    V = pltpu.VMEM
    tile = (fields, 128)
    coarse_out, fine_out = pl.pallas_call(
        functools.partial(
            kernel, lax.axis_size("gx"), lax.axis_size("gy"), fields, size_x, slots
        ),
        out_shape=(
            jax.ShapeDtypeStruct((flat, merged), F32),
            jax.ShapeDtypeStruct((slots, flat, fine_merged), F32),
        ),
        in_specs=[smem, smem, any_spec, any_spec, any_spec, any_spec, vmem, vmem],
        out_specs=(any_spec, any_spec),
        scratch_shapes=[
            V((flat, 128), F32),
            V((size_x, 128), F32),
            V((slots, 2, flat, 128), F32),
            V((slots, size_x, fine_merged), F32),
            V((slots, 2, flat, 128), F32),
            V((flat, 128), F32),
            V((slots, size_x + 2, fields, fine_merged), F32),
            V((slots, size_x + 2, fields, fine_merged), F32),
            V((2, 2) + tile, F32),
            V((2, 2) + tile, F32),
            V((2, 2) + tile, F32),
            V((2, 2) + tile, F32),
            V((size_x,) + tile, F32),
            V((2, 2) + tile, F32),
            V((2, 2, 2) + tile, F32),
            V((2, 2, 2) + tile, F32),
            V((2, 2, 2) + tile, F32),
            V((slots, size_x // 2) + tile, F32),
            V((2, size_x // 4) + tile, F32),
            V((2, size_x // 4) + tile, F32),
            V((4 * fields, 3 * fields), BF16),
            V((4 * fields, 3 * fields), BF16),
            V((slots, size_x, 8, fine_merged), F32),
            pltpu.SemaphoreType.DMA((11,)),
            pltpu.SemaphoreType.DMA((9,)),
            pltpu.SemaphoreType.DMA((12,)),
            pltpu.SemaphoreType.DMA((12,)),
        ],
        compiler_params=pltpu.CompilerParams(
            collective_id=0, has_side_effects=True, vmem_limit_bytes=67043328
        ),
    )(
        refine_to, parent_of, coarse_state.reshape(flat, merged), coarse_rate,
        fine_state.reshape(slots, flat, fine_merged), fine_rate, kappa.reshape(1, fields), reaction,
    )
    return coarse_out.reshape(coarse_state.shape), fine_out.reshape(fine_state.shape)


def solution(mesh):
    in_specs = (
        P(None, "gx", "gy"),
        P("gx", "gy"),
        P(("gx", "gy"), None, None, None),
        P(("gx", "gy"), None, None),
        P(("gx", "gy")),
        P(("gx", "gy")),
        P(),
        P(),
    )
    out_specs = (P(None, "gx", "gy"), P(("gx", "gy"), None, None, None))
    return jax.shard_map(body, mesh=mesh, in_specs=in_specs, out_specs=out_specs, check_vma=False)
```

```python
import functools
import jax
import jax.numpy as jnp
from jax import lax
from jax.experimental import pallas as pl
from jax.experimental.pallas import tpu as pltpu
from jax.sharding import PartitionSpec as P

MESH = pl.DeviceIdType.MESH
F32 = jnp.float32
BF16 = jnp.bfloat16


def lanes(rows):
    return lax.broadcasted_iota(jnp.int32, (rows, 128), 1)


def pick(table, index):
    return jnp.take_along_axis(table, index, axis=1)


def powers(reaction, fields):
    row = lax.broadcasted_iota(jnp.int32, (fields, 3 * fields), 0)
    col = lax.broadcasted_iota(jnp.int32, (fields, 3 * fields), 1)
    power = (col % fields == row).astype(F32)
    result = []
    for _ in range(4):
        power = jnp.dot(
            reaction, power, precision=lax.Precision.HIGHEST, preferred_element_type=F32
        )
        result.append(power)
    return result, col < 2 * fields


def chem_weights(power_list, high_part, step):
    parts = []
    for count, (choose, power) in enumerate(zip((4.0, 6.0, 4.0, 1.0), power_list)):
        value = power * (choose * step ** (count + 1))
        high = value.astype(BF16).astype(F32)
        parts.append(jnp.where(high_part, high, value - high))
    return jnp.concatenate(parts, axis=0).astype(BF16)


def chemistry(weights, values, rates, fields):
    wide = jnp.concatenate(values, axis=1)
    high = wide.astype(BF16).astype(F32)
    low = wide - high
    stacked = jnp.concatenate([high, low, high], axis=0).astype(BF16)
    product = jnp.dot(weights, stacked, preferred_element_type=F32)
    out = []
    for n, (value, rate) in enumerate(zip(values, rates)):
        part = [
            product[q * fields : (q + 1) * fields, n * 128 : (n + 1) * 128] for q in range(4)
        ]
        rate = jnp.broadcast_to(rate, value.shape)
        out.append(value + rate * (part[0] + rate * (part[1] + rate * (part[2] + rate * part[3]))))
    return out


def kernel(
    n_gx, n_gy, fields, size_x, slots,
    refine_ref, parent_ref, coarse_hbm, crate_hbm, fine_hbm, frate_hbm, kappa_ref, reaction_ref,
    coarse_out_hbm, fine_out_hbm,
    cin, crate, fin, frate, fout, cout,
    buf_a, buf_b, row_send, col_send, hx, hy, cnew, cols, ring_local, ring_send, ring_recv,
    means, mean_send, mean_recv, wf_ref, wc_ref, rate8, edge_rate,
    in_sem, out_sem, send_sem, recv_sem,
):
    F = fields
    fine_cols = frate.shape[2]
    gx = lax.axis_index("gx")
    gy = lax.axis_index("gy")
    right = lax.rem(gx + 1, n_gx)
    left = lax.rem(gx + n_gx - 1, n_gx)
    above = lax.rem(gy + 1, n_gy)
    below = lax.rem(gy + n_gy - 1, n_gy)

    loads = [
        pltpu.make_async_copy(coarse_hbm, cin, in_sem.at[0]),
        pltpu.make_async_copy(crate_hbm, crate, in_sem.at[1]),
        pltpu.make_async_copy(frate_hbm, frate, in_sem.at[2]),
    ]
    fine_loads = []
    for s in range(slots):
        for h in range(2):
            fine_loads.append(
                pltpu.make_async_copy(
                    fine_hbm.at[s, :, pl.ds(h * 128, 128)], fin.at[s, h], in_sem.at[3 + 2 * s + h]
                )
            )
    for copy in loads + fine_loads:
        copy.start()

    barrier = pltpu.get_barrier_semaphore()
    for target in ((left, gy), (right, gy), (gx, below), (gx, above)):
        pl.semaphore_signal(barrier, inc=1, device_id=target, device_id_type=MESH)

    def send(n, src, dst, target):
        copy = pltpu.make_async_remote_copy(
            src_ref=src, dst_ref=dst, send_sem=send_sem.at[n], recv_sem=recv_sem.at[n],
            device_id=target, device_id_type=MESH,
        )
        copy.start()
        return copy

    lane = lanes(F)
    first_half = lane < 64

    def pack(rows_of, y):
        total = jnp.zeros((F, 128), F32)
        for x in range(size_x):
            shift = ((x - y) * 8) % 128
            row = rows_of(x)
            moved = pltpu.roll(row, shift, 1) if shift else row
            total = jnp.where(lane // 8 == x, moved, total)
        return total

    def halos(level):
        base = 4 * level
        return [
            send(base + 0, row_send.at[level, 1], hx.at[level, 0], (right, gy)),
            send(base + 1, row_send.at[level, 0], hx.at[level, 1], (left, gy)),
            send(base + 2, col_send.at[level, 1], hy.at[level, 0], (gx, above)),
            send(base + 3, col_send.at[level, 0], hy.at[level, 1], (gx, below)),
        ]

    loads[0].wait()
    old_rows = lambda x: cin[pl.ds(x, F, stride=size_x), :]
    row_send[0, 0] = old_rows(0)
    row_send[0, 1] = old_rows(size_x - 1)
    col_send[0, 0] = pack(old_rows, 0)
    col_send[0, 1] = pack(old_rows, size_x - 1)

    cols[0, 0] = pack(old_rows, size_x // 2 - 1)
    cols[0, 1] = pack(old_rows, size_x // 2)
    power_list, high_part = powers(reaction_ref[...], F)
    wf_ref[...] = chem_weights(power_list, high_part, 0.125)
    wc_ref[...] = chem_weights(power_list, high_part, 0.25)
    diag = lax.broadcasted_iota(jnp.int32, (F, F), 0) == lax.broadcasted_iota(jnp.int32, (F, F), 1)
    kappa_col = jnp.sum(
        jnp.where(diag, jnp.broadcast_to(kappa_ref[...], (F, F)), 0.0), axis=1, keepdims=True
    )
    kappa = jnp.broadcast_to(kappa_col, (F, 128))
    kappa2 = 2.0 * kappa

    for copy in fine_loads:
        copy.wait()
    for s in range(slots):
        for h in range(2):
            for x in range(size_x):
                buf_a[s, x + 1, :, pl.ds(h * 128, 128)] = fin[s, h, pl.ds(x, F, stride=size_x), :]
    loads[1].wait()
    loads[2].wait()
    for s in range(slots):
        for x in range(size_x):
            rate8[s, x] = jnp.broadcast_to(frate[s, pl.ds(x, 1), :], rate8.shape[2:])
    lane8 = lanes(8)
    for s in range(slots):
        for q in range(size_x // 4):
            total = jnp.zeros((8, 128), F32)
            for n in range(4):
                lo = rate8[s, 4 * q + n, :, pl.ds(0, 128)]
                hi = rate8[s, 4 * q + n, :, pl.ds(fine_cols - 128, 128)]
                lo = pltpu.roll(lo, 16 * n, 1) if n else lo
                shift = (16 * n - 48) % 128
                hi = pltpu.roll(hi, shift, 1) if shift else hi
                total = jnp.where(lane8 // 16 == n, lo, total)
                total = jnp.where(lane8 // 16 == 4 + n, hi, total)
            edge_rate[s, q] = total
    z16 = lane % 16
    row_index = (lane // 32) * 8 + z16 // 2
    col_index = jnp.where(lane < 64, 0, 64) + z16 // 2
    target = lane % 64
    mean_index = ((target // 8) % 4) * 32 + 2 * (target % 8)
    mean_low = target // 32 == 0

    def ring_of(level, s, side):
        return ring_local[level, s, side] if s < 2 else ring_recv[level, s - 2, side]

    def fine_step(s, step):
        src = buf_a if step == 0 else buf_b
        if step == 0:
            src[s, 0] = jnp.zeros((F, fine_cols), F32)
            src[s, size_x + 1] = jnp.zeros((F, fine_cols), F32)
        else:
            edge_x = 0.5 * (ring_of(0, s, 0) + ring_of(1, s, 0))
            edge_y = 0.5 * (ring_of(0, s, 1) + ring_of(1, s, 1))
            for h in range(2):
                src[s, 0, :, pl.ds(h * 128, 128)] = pick(edge_x, row_index + 32 * h)
                src[s, size_x + 1, :, pl.ds(h * 128, 128)] = pick(edge_x, row_index + 64 + 32 * h)
        weights = wf_ref[...]
        live = jnp.full((F, 128), parent_ref[s], jnp.int32) >= 0

        def pair(j, carry):
            ghost = pick(edge_y, col_index + 8 * j) if step else jnp.zeros((F, 128), F32)
            values, rates = [], []
            for n in range(2):
                x = 2 * j + n
                c = [src[s, x + 1, :, pl.ds(h * 128, 128)] for h in range(2)]
                up = [src[s, x, :, pl.ds(h * 128, 128)] for h in range(2)]
                dn = [src[s, x + 2, :, pl.ds(h * 128, 128)] for h in range(2)]
                ra = [pltpu.roll(v, 16, 1) for v in c]
                rb = [pltpu.roll(v, 112, 1) for v in c]
                yl = [jnp.where(lane < 16, ghost, ra[0]), jnp.where(lane < 16, ra[0], ra[1])]
                yh = [jnp.where(lane >= 112, rb[1], rb[0]), jnp.where(lane >= 112, ghost, rb[1])]
                for h in range(2):
                    v = c[h]
                    zl = jnp.where(z16 == 0, pltpu.roll(v, 113, 1), pltpu.roll(v, 1, 1))
                    zu = jnp.where(z16 == 15, pltpu.roll(v, 15, 1), pltpu.roll(v, 127, 1))
                    lap = (yl[h] + yh[h]) + (up[h] + dn[h]) + (zl + zu) - 6.0 * v
                    values.append(v + kappa2 * lap - 0.25 * (v - zl))
                    rate = rate8[s, x, :, pl.ds(h * 128, 128)]
                    rates.append(jnp.concatenate([rate] * (F // 8), axis=0))
            new = chemistry(weights, values, rates, F)
            if step == 0:
                for n in range(2):
                    for h in range(2):
                        buf_b[s, 2 * j + n + 1, :, pl.ds(h * 128, 128)] = new[2 * n + h]
            else:
                new = [jnp.where(live, v, 0.0) for v in new]
                for n in range(2):
                    for h in range(2):
                        fout[s, h, pl.ds(2 * j + n, F, stride=size_x), :] = new[2 * n + h]
                picked = []
                for h in range(2):
                    total = new[h] + new[2 + h]
                    total = total + pltpu.roll(total, 127, 1)
                    total = total + pltpu.roll(total, 112, 1)
                    picked.append(pick(total, mean_index))
                means[s, j] = 0.125 * jnp.where(mean_low, picked[0], picked[1])
            return carry

        lax.fori_loop(0, size_x // 2, pair, 0, unroll=4)

    edge_index = (lane // 64) * 64 + ((lane % 64) // 32) * 8 + z16 // 2

    def wide_rate(rate):
        return jnp.concatenate([rate] * (F // 8), axis=0)

    def correct(s):
        edge_x, edge_y = ring_of(0, s, 0), ring_of(0, s, 1)
        values, rates = [], []
        for side, x in ((0, 0), (1, size_x - 1)):
            for h in range(2):
                values.append(kappa2 * pick(edge_x, row_index + 64 * side + 32 * h))
                rates.append(wide_rate(rate8[s, x, :, pl.ds(h * 128, 128)]))
        for q in range(size_x // 4):
            values.append(kappa2 * pick(edge_y, edge_index + 16 * q))
            rates.append(wide_rate(edge_rate[s, q]))
        share = chemistry(wf_ref[...], values, rates, F)
        for x in range(size_x):
            q, n = x // 4, x % 4
            both = share[4 + q]
            lo = pltpu.roll(both, (-16 * n) % 128, 1) if n else both
            shift = (48 - 16 * n) % 128
            hi = pltpu.roll(both, shift, 1) if shift else both
            added = [jnp.where(lane < 16, lo, 0.0), jnp.where(lane >= 112, hi, 0.0)]
            for h in range(2):
                if x == 0:
                    added[h] = added[h] + share[h]
                if x == size_x - 1:
                    added[h] = added[h] + share[2 + h]
                here = (s, x + 1, slice(None), pl.ds(h * 128, 128))
                buf_b[here] = buf_b[here] + added[h]

    for s in ():
        fine_step(s, 0)
    pl.semaphore_wait(barrier, 4)
    old_halos = halos(0)
    for s in (0, 1):
        fine_step(s, 0)
    for copy in old_halos:
        copy.wait_recv()

    z8 = lane % 8
    for group in range(size_x // 4):
        values, rates = [], []
        for x in range(4 * group, 4 * group + 4):
            c = old_rows(x)
            up = old_rows(x - 1) if x > 0 else hx[0, 0]
            dn = old_rows(x + 1) if x < size_x - 1 else hx[0, 1]
            ghost_lo = pltpu.roll(hy[0, 0], (-x * 8) % 128, 1) if x else hy[0, 0]
            shift = (120 - x * 8) % 128
            ghost_hi = pltpu.roll(hy[0, 1], shift, 1) if shift else hy[0, 1]
            yl = jnp.where(lane < 8, ghost_lo, pltpu.roll(c, 8, 1))
            yh = jnp.where(lane >= 120, ghost_hi, pltpu.roll(c, 120, 1))
            zl = jnp.where(z8 == 0, pltpu.roll(c, 121, 1), pltpu.roll(c, 1, 1))
            zu = jnp.where(z8 == 7, pltpu.roll(c, 7, 1), pltpu.roll(c, 127, 1))
            lap = (yl + yh) + (up + dn) + (zl + zu) - 6.0 * c
            values.append(c + kappa * lap - 0.25 * (c - zl))
            rates.append(crate[pl.ds(x, 1), :])
        for n, new in enumerate(chemistry(wc_ref[...], values, rates, F)):
            cnew[4 * group + n] = new
    new_rows = lambda x: cnew[x]
    row_send[1, 0] = new_rows(0)
    row_send[1, 1] = new_rows(size_x - 1)
    col_send[1, 0] = pack(new_rows, 0)
    col_send[1, 1] = pack(new_rows, size_x - 1)
    new_halos = halos(1)

    parents = [jnp.full((F, 128), refine_ref[p], jnp.int32) for p in range(4)]

    def rings(level, rows_of):
        mid = size_x // 2
        row_at = (hx[level, 0], rows_of(mid - 1), rows_of(mid), hx[level, 1])
        col_at = (hy[level, 0], cols[level, 0], cols[level, 1], hy[level, 1])

        def joined(lo, hi, half):
            if half == 0:
                return jnp.where(first_half, lo, pltpu.roll(hi, 64, 1))
            return jnp.where(first_half, pltpu.roll(lo, 64, 1), hi)

        all_rings = []
        for p in range(4):
            a, b = p // 2, p % 2
            all_rings.append(
                (joined(row_at[a], row_at[a + 2], b), joined(col_at[b], col_at[b + 2], a))
            )
        for k in range(4):
            for side in range(2):
                value = jnp.zeros((F, 128), F32)
                for p in range(4):
                    value = jnp.where(parents[p] == k, all_rings[p][side], value)
                if k < 2:
                    ring_local[level, k, side] = value
                else:
                    ring_send[level, k - 2, side] = value
        return send(8 + level, ring_send.at[level], ring_recv.at[level], (right, gy))

    ring_old = rings(0, old_rows)
    cols[1, 0] = pack(new_rows, size_x // 2 - 1)
    cols[1, 1] = pack(new_rows, size_x // 2)

    stores = []

    def store(s):
        for h in range(2):
            copy = pltpu.make_async_copy(
                fout.at[s, h], fine_out_hbm.at[s, :, pl.ds(h * 128, 128)], out_sem.at[2 * s + h]
            )
            copy.start()
            stores.append(copy)

    half = size_x // 4

    def send_means(s):
        for j in range(half):
            mean_send[s - 2, j] = jnp.where(first_half, means[s, j], means[s, j + half])
        return send(8 + s, mean_send.at[s - 2], mean_recv.at[s - 2], (left, gy))

    for s in (2, 3):
        fine_step(s, 0)
    correct(0)
    correct(1)
    for copy in new_halos:
        copy.wait_recv()
    ring_new = rings(1, new_rows)
    fine_step(0, 1)
    store(0)
    ring_old.wait_recv()
    correct(2)
    correct(3)
    ring_new.wait_recv()
    fine_step(2, 1)
    sent_2 = send_means(2)
    store(2)
    fine_step(3, 1)
    sent_3 = send_means(3)
    store(3)
    fine_step(1, 1)
    store(1)
    sent_2.wait_recv()
    sent_3.wait_recv()

    for x in range(size_x):
        a, X = x // (size_x // 2), x % (size_x // 2)
        full = [means[0, X], means[1, X]]
        for k in range(2):
            packed = mean_recv[k, X % half]
            turned = pltpu.roll(packed, 64, 1)
            low, high = (packed, turned) if X < half else (turned, packed)
            full.append(jnp.where(first_half, low, high))
        owner = jnp.where(first_half, parents[2 * a], parents[2 * a + 1])
        value = new_rows(x)
        for k in range(4):
            value = jnp.where(owner == k, full[k], value)
        cout[pl.ds(x, F, stride=size_x), :] = value
    last = pltpu.make_async_copy(cout, coarse_out_hbm, out_sem.at[8])
    last.start()
    stores.append(last)
    for copy in old_halos + new_halos + [ring_old, ring_new, sent_2, sent_3]:
        copy.wait_send()
    for copy in stores:
        copy.wait()


def body(coarse_state, coarse_rate, fine_state, fine_rate, refine_to, parent_of, kappa, reaction):
    fields, size_x, merged = coarse_state.shape
    slots = fine_state.shape[0]
    fine_merged = fine_state.shape[3]
    flat = fields * size_x
    any_spec = pl.BlockSpec(memory_space=pl.ANY)
    smem = pl.BlockSpec(memory_space=pltpu.SMEM)
    vmem = pl.BlockSpec(memory_space=pltpu.VMEM)
    V = pltpu.VMEM
    tile = (fields, 128)
    coarse_out, fine_out = pl.pallas_call(
        functools.partial(
            kernel, lax.axis_size("gx"), lax.axis_size("gy"), fields, size_x, slots
        ),
        out_shape=(
            jax.ShapeDtypeStruct((flat, merged), F32),
            jax.ShapeDtypeStruct((slots, flat, fine_merged), F32),
        ),
        in_specs=[smem, smem, any_spec, any_spec, any_spec, any_spec, vmem, vmem],
        out_specs=(any_spec, any_spec),
        scratch_shapes=[
            V((flat, 128), F32),
            V((size_x, 128), F32),
            V((slots, 2, flat, 128), F32),
            V((slots, size_x, fine_merged), F32),
            V((slots, 2, flat, 128), F32),
            V((flat, 128), F32),
            V((slots, size_x + 2, fields, fine_merged), F32),
            V((slots, size_x + 2, fields, fine_merged), F32),
            V((2, 2) + tile, F32),
            V((2, 2) + tile, F32),
            V((2, 2) + tile, F32),
            V((2, 2) + tile, F32),
            V((size_x,) + tile, F32),
            V((2, 2) + tile, F32),
            V((2, 2, 2) + tile, F32),
            V((2, 2, 2) + tile, F32),
            V((2, 2, 2) + tile, F32),
            V((slots, size_x // 2) + tile, F32),
            V((2, size_x // 4) + tile, F32),
            V((2, size_x // 4) + tile, F32),
            V((4 * fields, 3 * fields), BF16),
            V((4 * fields, 3 * fields), BF16),
            V((slots, size_x, 8, fine_merged), F32),
            V((slots, size_x // 4, 8, 128), F32),
            pltpu.SemaphoreType.DMA((11,)),
            pltpu.SemaphoreType.DMA((9,)),
            pltpu.SemaphoreType.DMA((12,)),
            pltpu.SemaphoreType.DMA((12,)),
        ],
        compiler_params=pltpu.CompilerParams(
            collective_id=0, has_side_effects=True, vmem_limit_bytes=67043328
        ),
    )(
        refine_to, parent_of, coarse_state.reshape(flat, merged), coarse_rate,
        fine_state.reshape(slots, flat, fine_merged), fine_rate, kappa.reshape(1, fields), reaction,
    )
    return coarse_out.reshape(coarse_state.shape), fine_out.reshape(fine_state.shape)


def solution(mesh):
    in_specs = (
        P(None, "gx", "gy"),
        P("gx", "gy"),
        P(("gx", "gy"), None, None, None),
        P(("gx", "gy"), None, None),
        P(("gx", "gy")),
        P(("gx", "gy")),
        P(),
        P(),
    )
    out_specs = (P(None, "gx", "gy"), P(("gx", "gy"), None, None, None))
    return jax.shard_map(body, mesh=mesh, in_specs=in_specs, out_specs=out_specs, check_vma=False)
```

```python
import functools
import jax
import jax.numpy as jnp
from jax import lax
from jax.experimental import pallas as pl
from jax.experimental.pallas import tpu as pltpu
from jax.sharding import PartitionSpec as P

MESH = pl.DeviceIdType.MESH
F32 = jnp.float32
BF16 = jnp.bfloat16


def lanes(rows):
    return lax.broadcasted_iota(jnp.int32, (rows, 128), 1)


def pick(table, index):
    return jnp.take_along_axis(table, index, axis=1)


def powers(reaction, fields):
    row = lax.broadcasted_iota(jnp.int32, (fields, 3 * fields), 0)
    col = lax.broadcasted_iota(jnp.int32, (fields, 3 * fields), 1)
    power = (col % fields == row).astype(F32)
    result = []
    for _ in range(4):
        power = jnp.dot(
            reaction, power, precision=lax.Precision.HIGHEST, preferred_element_type=F32
        )
        result.append(power)
    return result, col < 2 * fields


def chem_weights(power_list, high_part, step):
    parts = []
    for count, (choose, power) in enumerate(zip((4.0, 6.0, 4.0, 1.0), power_list)):
        value = power * (choose * step ** (count + 1))
        high = value.astype(BF16).astype(F32)
        parts.append(jnp.where(high_part, high, value - high))
    return jnp.concatenate(parts, axis=0).astype(BF16)


def chemistry(weights, values, rates, fields):
    wide = jnp.concatenate(values, axis=1)
    high = wide.astype(BF16).astype(F32)
    low = wide - high
    stacked = jnp.concatenate([high, low, high], axis=0).astype(BF16)
    product = jnp.dot(weights, stacked, preferred_element_type=F32)
    out = []
    for n, (value, rate) in enumerate(zip(values, rates)):
        part = [
            product[q * fields : (q + 1) * fields, n * 128 : (n + 1) * 128] for q in range(4)
        ]
        rate = jnp.broadcast_to(rate, value.shape)
        out.append(value + rate * (part[0] + rate * (part[1] + rate * (part[2] + rate * part[3]))))
    return out


def kernel(
    n_gx, n_gy, fields, size_x, slots,
    refine_ref, parent_ref, coarse_hbm, crate_hbm, fine_hbm, frate_hbm, kappa_ref, reaction_ref,
    coarse_out_hbm, fine_out_hbm,
    cin, crate, fin, frate, fout, cout,
    buf_a, buf_b, row_send, col_send, hx, hy, cnew, cols, ring_local, ring_send, ring_recv,
    means, mean_send, mean_recv, wf_ref, wc_ref, rate8, edge_rate,
    in_sem, out_sem, send_sem, recv_sem,
):
    F = fields
    fine_cols = frate.shape[2]
    gx = lax.axis_index("gx")
    gy = lax.axis_index("gy")
    right = lax.rem(gx + 1, n_gx)
    left = lax.rem(gx + n_gx - 1, n_gx)
    above = lax.rem(gy + 1, n_gy)
    below = lax.rem(gy + n_gy - 1, n_gy)

    loads = [
        pltpu.make_async_copy(coarse_hbm, cin, in_sem.at[0]),
        pltpu.make_async_copy(crate_hbm, crate, in_sem.at[1]),
        pltpu.make_async_copy(frate_hbm, frate, in_sem.at[2]),
    ]
    fine_loads = []
    for s in range(slots):
        for h in range(2):
            fine_loads.append(
                pltpu.make_async_copy(
                    fine_hbm.at[s, :, pl.ds(h * 128, 128)], fin.at[s, h], in_sem.at[3 + 2 * s + h]
                )
            )
    for copy in loads + fine_loads:
        copy.start()

    barrier = pltpu.get_barrier_semaphore()
    for target in ((left, gy), (right, gy), (gx, below), (gx, above)):
        pl.semaphore_signal(barrier, inc=1, device_id=target, device_id_type=MESH)

    def send(n, src, dst, target):
        copy = pltpu.make_async_remote_copy(
            src_ref=src, dst_ref=dst, send_sem=send_sem.at[n], recv_sem=recv_sem.at[n],
            device_id=target, device_id_type=MESH,
        )
        copy.start()
        return copy

    lane = lanes(F)
    first_half = lane < 64

    def pack(rows_of, y):
        total = jnp.zeros((F, 128), F32)
        for x in range(size_x):
            shift = ((x - y) * 8) % 128
            row = rows_of(x)
            moved = pltpu.roll(row, shift, 1) if shift else row
            total = jnp.where(lane // 8 == x, moved, total)
        return total

    def halos(level):
        base = 4 * level
        return [
            send(base + 0, row_send.at[level, 1], hx.at[level, 0], (right, gy)),
            send(base + 1, row_send.at[level, 0], hx.at[level, 1], (left, gy)),
            send(base + 2, col_send.at[level, 1], hy.at[level, 0], (gx, above)),
            send(base + 3, col_send.at[level, 0], hy.at[level, 1], (gx, below)),
        ]

    loads[0].wait()
    old_rows = lambda x: cin[pl.ds(x, F, stride=size_x), :]
    row_send[0, 0] = old_rows(0)
    row_send[0, 1] = old_rows(size_x - 1)
    col_send[0, 0] = pack(old_rows, 0)
    col_send[0, 1] = pack(old_rows, size_x - 1)

    cols[0, 0] = pack(old_rows, size_x // 2 - 1)
    cols[0, 1] = pack(old_rows, size_x // 2)
    power_list, high_part = powers(reaction_ref[...], F)
    wf_ref[...] = chem_weights(power_list, high_part, 0.125)
    wc_ref[...] = chem_weights(power_list, high_part, 0.25)
    diag = lax.broadcasted_iota(jnp.int32, (F, F), 0) == lax.broadcasted_iota(jnp.int32, (F, F), 1)
    kappa_col = jnp.sum(
        jnp.where(diag, jnp.broadcast_to(kappa_ref[...], (F, F)), 0.0), axis=1, keepdims=True
    )
    kappa = jnp.broadcast_to(kappa_col, (F, 128))
    kappa2 = 2.0 * kappa

    for copy in fine_loads:
        copy.wait()
    for s in range(slots):
        for h in range(2):
            for x in range(size_x):
                buf_a[s, x + 1, :, pl.ds(h * 128, 128)] = fin[s, h, pl.ds(x, F, stride=size_x), :]
    loads[1].wait()
    loads[2].wait()
    for s in range(slots):
        for x in range(size_x):
            rate8[s, x] = jnp.broadcast_to(frate[s, pl.ds(x, 1), :], rate8.shape[2:])
    lane8 = lanes(8)
    for s in range(slots):
        for q in range(size_x // 4):
            total = jnp.zeros((8, 128), F32)
            for n in range(4):
                lo = rate8[s, 4 * q + n, :, pl.ds(0, 128)]
                hi = rate8[s, 4 * q + n, :, pl.ds(fine_cols - 128, 128)]
                lo = pltpu.roll(lo, 16 * n, 1) if n else lo
                shift = (16 * n - 48) % 128
                hi = pltpu.roll(hi, shift, 1) if shift else hi
                total = jnp.where(lane8 // 16 == n, lo, total)
                total = jnp.where(lane8 // 16 == 4 + n, hi, total)
            edge_rate[s, q] = total
    z16 = lane % 16
    row_index = (lane // 32) * 8 + z16 // 2
    col_index = jnp.where(lane < 64, 0, 64) + z16 // 2
    target = lane % 64
    mean_index = ((target // 8) % 4) * 32 + 2 * (target % 8)
    mean_low = target // 32 == 0

    def ring_of(level, s, side):
        return ring_local[level, s, side] if s < 2 else ring_recv[level, s - 2, side]

    def fine_step(s, step):
        src = buf_a if step == 0 else buf_b
        if step == 0:
            src[s, 0] = jnp.zeros((F, fine_cols), F32)
            src[s, size_x + 1] = jnp.zeros((F, fine_cols), F32)
        else:
            edge_x = 0.5 * (ring_of(0, s, 0) + ring_of(1, s, 0))
            edge_y = 0.5 * (ring_of(0, s, 1) + ring_of(1, s, 1))
            for h in range(2):
                src[s, 0, :, pl.ds(h * 128, 128)] = pick(edge_x, row_index + 32 * h)
                src[s, size_x + 1, :, pl.ds(h * 128, 128)] = pick(edge_x, row_index + 64 + 32 * h)
        weights = wf_ref[...]
        live = jnp.full((F, 128), parent_ref[s], jnp.int32) >= 0

        own = 0.75 - 6.0 * kappa2

        def pair(j, carry):
            ghost = pick(edge_y, col_index + 8 * j) if step else jnp.zeros((F, 128), F32)
            values, rates = [], []
            for n in range(2):
                x = 2 * j + n
                c = [src[s, x + 1, :, pl.ds(h * 128, 128)] for h in range(2)]
                up = [src[s, x, :, pl.ds(h * 128, 128)] for h in range(2)]
                dn = [src[s, x + 2, :, pl.ds(h * 128, 128)] for h in range(2)]
                ra = [pltpu.roll(v, 16, 1) for v in c]
                rb = [pltpu.roll(v, 112, 1) for v in c]
                yl = [jnp.where(lane < 16, ghost, ra[0]), jnp.where(lane < 16, ra[0], ra[1])]
                yh = [jnp.where(lane >= 112, rb[1], rb[0]), jnp.where(lane >= 112, ghost, rb[1])]
                for h in range(2):
                    v = c[h]
                    zl = jnp.where(z16 == 0, pltpu.roll(v, 113, 1), pltpu.roll(v, 1, 1))
                    zu = jnp.where(z16 == 15, pltpu.roll(v, 15, 1), pltpu.roll(v, 127, 1))
                    near = (yl[h] + yh[h]) + (up[h] + dn[h]) + (zl + zu)
                    values.append(own * v + kappa2 * near + 0.25 * zl)
                    rate = rate8[s, x, :, pl.ds(h * 128, 128)]
                    rates.append(jnp.concatenate([rate] * (F // 8), axis=0))
            new = chemistry(weights, values, rates, F)
            if step == 0:
                for n in range(2):
                    for h in range(2):
                        buf_b[s, 2 * j + n + 1, :, pl.ds(h * 128, 128)] = new[2 * n + h]
            else:
                new = [jnp.where(live, v, 0.0) for v in new]
                for n in range(2):
                    for h in range(2):
                        fout[s, h, pl.ds(2 * j + n, F, stride=size_x), :] = new[2 * n + h]
                picked = []
                for h in range(2):
                    total = new[h] + new[2 + h]
                    total = total + pltpu.roll(total, 127, 1)
                    total = total + pltpu.roll(total, 112, 1)
                    picked.append(pick(total, mean_index))
                means[s, j] = 0.125 * jnp.where(mean_low, picked[0], picked[1])
            return carry

        lax.fori_loop(0, size_x // 2, pair, 0, unroll=4)

    edge_index = (lane // 64) * 64 + ((lane % 64) // 32) * 8 + z16 // 2

    def wide_rate(rate):
        return jnp.concatenate([rate] * (F // 8), axis=0)

    def correct(s):
        edge_x, edge_y = ring_of(0, s, 0), ring_of(0, s, 1)
        values, rates = [], []
        for side, x in ((0, 0), (1, size_x - 1)):
            for h in range(2):
                values.append(kappa2 * pick(edge_x, row_index + 64 * side + 32 * h))
                rates.append(wide_rate(rate8[s, x, :, pl.ds(h * 128, 128)]))
        for q in range(size_x // 4):
            values.append(kappa2 * pick(edge_y, edge_index + 16 * q))
            rates.append(wide_rate(edge_rate[s, q]))
        share = chemistry(wf_ref[...], values, rates, F)
        for x in range(size_x):
            q, n = x // 4, x % 4
            both = share[4 + q]
            lo = pltpu.roll(both, (-16 * n) % 128, 1) if n else both
            shift = (48 - 16 * n) % 128
            hi = pltpu.roll(both, shift, 1) if shift else both
            added = [jnp.where(lane < 16, lo, 0.0), jnp.where(lane >= 112, hi, 0.0)]
            for h in range(2):
                if x == 0:
                    added[h] = added[h] + share[h]
                if x == size_x - 1:
                    added[h] = added[h] + share[2 + h]
                here = (s, x + 1, slice(None), pl.ds(h * 128, 128))
                buf_b[here] = buf_b[here] + added[h]

    for s in ():
        fine_step(s, 0)
    pl.semaphore_wait(barrier, 4)
    old_halos = halos(0)
    for s in (0, 1):
        fine_step(s, 0)
    for copy in old_halos:
        copy.wait_recv()

    z8 = lane % 8
    for group in range(size_x // 4):
        values, rates = [], []
        for x in range(4 * group, 4 * group + 4):
            c = old_rows(x)
            up = old_rows(x - 1) if x > 0 else hx[0, 0]
            dn = old_rows(x + 1) if x < size_x - 1 else hx[0, 1]
            ghost_lo = pltpu.roll(hy[0, 0], (-x * 8) % 128, 1) if x else hy[0, 0]
            shift = (120 - x * 8) % 128
            ghost_hi = pltpu.roll(hy[0, 1], shift, 1) if shift else hy[0, 1]
            yl = jnp.where(lane < 8, ghost_lo, pltpu.roll(c, 8, 1))
            yh = jnp.where(lane >= 120, ghost_hi, pltpu.roll(c, 120, 1))
            zl = jnp.where(z8 == 0, pltpu.roll(c, 121, 1), pltpu.roll(c, 1, 1))
            zu = jnp.where(z8 == 7, pltpu.roll(c, 7, 1), pltpu.roll(c, 127, 1))
            lap = (yl + yh) + (up + dn) + (zl + zu) - 6.0 * c
            values.append(c + kappa * lap - 0.25 * (c - zl))
            rates.append(crate[pl.ds(x, 1), :])
        for n, new in enumerate(chemistry(wc_ref[...], values, rates, F)):
            cnew[4 * group + n] = new
    new_rows = lambda x: cnew[x]
    row_send[1, 0] = new_rows(0)
    row_send[1, 1] = new_rows(size_x - 1)
    col_send[1, 0] = pack(new_rows, 0)
    col_send[1, 1] = pack(new_rows, size_x - 1)
    new_halos = halos(1)

    parents = [jnp.full((F, 128), refine_ref[p], jnp.int32) for p in range(4)]

    def rings(level, rows_of):
        mid = size_x // 2
        row_at = (hx[level, 0], rows_of(mid - 1), rows_of(mid), hx[level, 1])
        col_at = (hy[level, 0], cols[level, 0], cols[level, 1], hy[level, 1])

        def joined(lo, hi, half):
            if half == 0:
                return jnp.where(first_half, lo, pltpu.roll(hi, 64, 1))
            return jnp.where(first_half, pltpu.roll(lo, 64, 1), hi)

        all_rings = []
        for p in range(4):
            a, b = p // 2, p % 2
            all_rings.append(
                (joined(row_at[a], row_at[a + 2], b), joined(col_at[b], col_at[b + 2], a))
            )
        for k in range(4):
            for side in range(2):
                value = jnp.zeros((F, 128), F32)
                for p in range(4):
                    value = jnp.where(parents[p] == k, all_rings[p][side], value)
                if k < 2:
                    ring_local[level, k, side] = value
                else:
                    ring_send[level, k - 2, side] = value
        return send(8 + level, ring_send.at[level], ring_recv.at[level], (right, gy))

    ring_old = rings(0, old_rows)
    cols[1, 0] = pack(new_rows, size_x // 2 - 1)
    cols[1, 1] = pack(new_rows, size_x // 2)

    stores = []

    def store(s):
        for h in range(2):
            copy = pltpu.make_async_copy(
                fout.at[s, h], fine_out_hbm.at[s, :, pl.ds(h * 128, 128)], out_sem.at[2 * s + h]
            )
            copy.start()
            stores.append(copy)

    half = size_x // 4

    def send_means(s):
        for j in range(half):
            mean_send[s - 2, j] = jnp.where(first_half, means[s, j], means[s, j + half])
        return send(8 + s, mean_send.at[s - 2], mean_recv.at[s - 2], (left, gy))

    for s in (2, 3):
        fine_step(s, 0)
    correct(0)
    correct(1)
    for copy in new_halos:
        copy.wait_recv()
    ring_new = rings(1, new_rows)
    fine_step(0, 1)
    store(0)
    ring_old.wait_recv()
    correct(2)
    correct(3)
    ring_new.wait_recv()
    fine_step(2, 1)
    sent_2 = send_means(2)
    store(2)
    fine_step(3, 1)
    sent_3 = send_means(3)
    store(3)
    fine_step(1, 1)
    store(1)
    sent_2.wait_recv()
    sent_3.wait_recv()

    for x in range(size_x):
        a, X = x // (size_x // 2), x % (size_x // 2)
        full = [means[0, X], means[1, X]]
        for k in range(2):
            packed = mean_recv[k, X % half]
            turned = pltpu.roll(packed, 64, 1)
            low, high = (packed, turned) if X < half else (turned, packed)
            full.append(jnp.where(first_half, low, high))
        owner = jnp.where(first_half, parents[2 * a], parents[2 * a + 1])
        value = new_rows(x)
        for k in range(4):
            value = jnp.where(owner == k, full[k], value)
        cout[pl.ds(x, F, stride=size_x), :] = value
    last = pltpu.make_async_copy(cout, coarse_out_hbm, out_sem.at[8])
    last.start()
    stores.append(last)
    for copy in old_halos + new_halos + [ring_old, ring_new, sent_2, sent_3]:
        copy.wait_send()
    for copy in stores:
        copy.wait()


def body(coarse_state, coarse_rate, fine_state, fine_rate, refine_to, parent_of, kappa, reaction):
    fields, size_x, merged = coarse_state.shape
    slots = fine_state.shape[0]
    fine_merged = fine_state.shape[3]
    flat = fields * size_x
    any_spec = pl.BlockSpec(memory_space=pl.ANY)
    smem = pl.BlockSpec(memory_space=pltpu.SMEM)
    vmem = pl.BlockSpec(memory_space=pltpu.VMEM)
    V = pltpu.VMEM
    tile = (fields, 128)
    coarse_out, fine_out = pl.pallas_call(
        functools.partial(
            kernel, lax.axis_size("gx"), lax.axis_size("gy"), fields, size_x, slots
        ),
        out_shape=(
            jax.ShapeDtypeStruct((flat, merged), F32),
            jax.ShapeDtypeStruct((slots, flat, fine_merged), F32),
        ),
        in_specs=[smem, smem, any_spec, any_spec, any_spec, any_spec, vmem, vmem],
        out_specs=(any_spec, any_spec),
        scratch_shapes=[
            V((flat, 128), F32),
            V((size_x, 128), F32),
            V((slots, 2, flat, 128), F32),
            V((slots, size_x, fine_merged), F32),
            V((slots, 2, flat, 128), F32),
            V((flat, 128), F32),
            V((slots, size_x + 2, fields, fine_merged), F32),
            V((slots, size_x + 2, fields, fine_merged), F32),
            V((2, 2) + tile, F32),
            V((2, 2) + tile, F32),
            V((2, 2) + tile, F32),
            V((2, 2) + tile, F32),
            V((size_x,) + tile, F32),
            V((2, 2) + tile, F32),
            V((2, 2, 2) + tile, F32),
            V((2, 2, 2) + tile, F32),
            V((2, 2, 2) + tile, F32),
            V((slots, size_x // 2) + tile, F32),
            V((2, size_x // 4) + tile, F32),
            V((2, size_x // 4) + tile, F32),
            V((4 * fields, 3 * fields), BF16),
            V((4 * fields, 3 * fields), BF16),
            V((slots, size_x, 8, fine_merged), F32),
            V((slots, size_x // 4, 8, 128), F32),
            pltpu.SemaphoreType.DMA((11,)),
            pltpu.SemaphoreType.DMA((9,)),
            pltpu.SemaphoreType.DMA((12,)),
            pltpu.SemaphoreType.DMA((12,)),
        ],
        compiler_params=pltpu.CompilerParams(
            collective_id=0, has_side_effects=True, vmem_limit_bytes=67043328
        ),
    )(
        refine_to, parent_of, coarse_state.reshape(flat, merged), coarse_rate,
        fine_state.reshape(slots, flat, fine_merged), fine_rate, kappa.reshape(1, fields), reaction,
    )
    return coarse_out.reshape(coarse_state.shape), fine_out.reshape(fine_state.shape)


def solution(mesh):
    in_specs = (
        P(None, "gx", "gy"),
        P("gx", "gy"),
        P(("gx", "gy"), None, None, None),
        P(("gx", "gy"), None, None),
        P(("gx", "gy")),
        P(("gx", "gy")),
        P(),
        P(),
    )
    out_specs = (P(None, "gx", "gy"), P(("gx", "gy"), None, None, None))
    return jax.shard_map(body, mesh=mesh, in_specs=in_specs, out_specs=out_specs, check_vma=False)
```
